32 devices in a mesh: groups: 2 (over y), hist: 4 (over z), tower: 2 (over x), head: 2 (over core).
Axes of the slice: x: 2, y: 2, z: 4, core: 2. Of those that a mesh axis runs over, the one named last changes fastest.
Arguments:
- queries: bfloat16 [1024, 1024], P(('groups', 'hist', 'tower'), 'head'), parts along dimension 0, may hold values from -6 to 6
- hist_keys: bfloat16 [4, 1024, 1024], P('groups', 'hist', 'head'), parts along dimension 0, may hold values from -6 to 6
- hist_values: bfloat16 [4, 1024, 1024], P('groups', 'hist', 'head'), parts along dimension 0, may hold values from -6 to 6
- cand_user: int32 [1024], P(('groups', 'hist', 'tower')), parts along dimension 0, may hold values from 0 to 1
- time_bucket: int32 [4, 1024], P('groups', 'hist'), parts along dimension 0, may hold values from 0 to 127
- hist_len: int32 [4], P('groups'), parts along dimension 0, may hold values from 256 to 1024
- cand_gate: bfloat16 [1024, 1024], P(('groups', 'hist', 'tower'), 'head'), parts along dimension 0, may hold values from -6 to 6
- time_bias: float32 [128, 8], P(None, 'head'), may hold values from -4 to 4
- tower_in: bfloat16 [1024, 4096], P('head', 'tower'), may hold values from -0.1875 to 0.1875
- tower_bias: float32 [4096], P('tower'), may hold values from -4 to 4
- tower_out: float32 [4096], P('tower'), may hold values from -0.09375 to 0.09375
Outputs:
- cand_states: bfloat16 [1024, 1024], P(('groups', 'hist', 'tower'), 'head'), parts along dimension 0
- cand_scores: float32 [1024], P(('groups', 'hist', 'tower')), parts along dimension 0
The draws below stay inside these ranges and needn't reach their ends.
There are 2 independent parts, one for each index of `groups`. The reference program is written for one: setup_inputs(seed, part) draws one part's arguments, and reference() takes and returns one part's arrays. A program takes and returns all parts, laid end to end along the dimension named above; an argument that names none is the same for every part. Nothing has to cross between parts.
All inputs are finite; a program needn't handle non-finite values.
Results may differ from the reference program's by a relative error of at most 0.017.
Values may be sent and summed in bfloat16 or wider, within the bound.
A program may use at most 64 MiB of HBM per device.

```python
import jax
import jax.numpy as jnp
from jax import lax

D = 1024
H = 8
DH = 128
FF = 4096
NB = 128
USERS = 2
HL_DEV = 256
HLEN = 1024
CANDS = 512
N_HIST = 4


def set_ends(entries, stream_key, low, largest):
    longest = entries.shape.index(max(entries.shape))
    spots = []
    for shift in (0, 1):
        where = [jax.random.randint(jax.random.fold_in(stream_key, axis), (), 0, length) for axis, length in enumerate(entries.shape)]
        where[longest] = (where[longest] + shift) % entries.shape[longest]
        spots.append(tuple(where))
    return entries.at[spots[0]].set(low).at[spots[1]].set(largest)


def steps_of(rng, dims, pieces, least, top_value):
    level, own = 1.0, jax.random.fold_in(rng, 6)
    for position, shards_of in pieces:
        steps = jnp.exp(jax.random.uniform(jax.random.fold_in(own, position), (shards_of,), jnp.float32, least / len(pieces), top_value / len(pieces)))
        level = level * jnp.repeat(steps, dims[position] // shards_of).reshape([-1 if axis == position else 1 for axis in range(len(dims))])
    return level


def centred(own_key, shape, scale, reach, pieces=(), kind=jnp.bfloat16):
    drawn = jax.random.normal(own_key, shape, jnp.float32) * scale
    if len(pieces) > 0:
        drawn = steps_of(own_key, shape, pieces, -0.22, 0.18) * drawn
    return jnp.clip(drawn, min=-reach, max=reach).astype(kind)


def setup_inputs(seed: int = 0, part: int = 0) -> dict:
    keys = jax.random.split(jax.random.key(seed), 12)
    part_splits = jax.random.split(jax.random.fold_in(keys[11], part), 12)
    return {
        "queries": centred(part_splits[0], (CANDS, D), 1.0, 6.0, ((0, 8), (1, 2))),
        "hist_keys": centred(part_splits[1], (USERS, HLEN, D), 1.0, 6.0, ((1, 4), (2, 2))),
        "hist_values": centred(part_splits[2], (USERS, HLEN, D), 1.0, 6.0, ((1, 4), (2, 2))),
        "cand_user": set_ends(jax.random.randint(part_splits[3], (CANDS,), 0, USERS), jax.random.fold_in(part_splits[3], 1), 0, USERS - 1).astype(jnp.int32),
        "time_bucket": set_ends(jax.random.randint(part_splits[4], (USERS, HLEN), 0, NB), jax.random.fold_in(part_splits[4], 1), 0, NB - 1).astype(jnp.int32),
        "hist_len": jax.random.randint(part_splits[5], (USERS,), HLEN // 4, HLEN + 1).astype(jnp.int32),
        "cand_gate": centred(part_splits[6], (CANDS, D), 1.0, 6.0, ((0, 8), (1, 2))),
        "time_bias": centred(keys[7], (NB, H), 1.0, 4.0, ((1, 2),), jnp.float32),
        "tower_in": centred(keys[8], (D, FF), D ** -0.5, 0.1875, ((0, 2), (1, 2))),
        "tower_bias": centred(keys[9], (FF,), 1.0, 4.0, ((0, 2),), jnp.float32),
        "tower_out": centred(keys[10], (FF,), FF ** -0.5, 0.09375, ((0, 2),), jnp.float32),
    }


def reference(queries, hist_keys, hist_values, cand_user, time_bucket, hist_len, cand_gate, time_bias, tower_in, tower_bias, tower_out):
    score_scale = DH ** (-0.5)
    positions = jnp.arange(HLEN, dtype=jnp.int32)
    key_live = positions[None, :] < hist_len[:, None]
    event_bias = time_bias[time_bucket]
    user_ids = jnp.arange(USERS, dtype=jnp.int32)
    shard_keys = jnp.swapaxes(hist_keys.reshape(USERS, N_HIST, HL_DEV, D), 0, 1)
    shard_values = jnp.swapaxes(hist_values.reshape(USERS, N_HIST, HL_DEV, D), 0, 1)
    shard_bias = jnp.swapaxes(event_bias.reshape(USERS, N_HIST, HL_DEV, H), 0, 1)
    shard_live = jnp.swapaxes(key_live.reshape(USERS, N_HIST, HL_DEV), 0, 1)

    def one_user(total, inputs):
        user_keys, user_values, user_bias, user_live, user_id = inputs
        same_user = jnp.where((cand_user == user_id)[:, None] & user_live[None, :], 1.0, 0.0).astype(jnp.float32)
        head_outputs = []
        for head_index in range(H):
            first = head_index * DH
            logits = lax.dot_general(queries[:, first:first + DH], user_keys[:, first:first + DH], (((1,), (1,)), ((), ())), preferred_element_type=jnp.float32)
            logits = logits * score_scale + user_bias[:, head_index][None, :]
            weights_bf = (jax.nn.silu(logits) * same_user).astype(jnp.bfloat16)
            head_outputs.append(jnp.dot(weights_bf, user_values[:, first:first + DH], preferred_element_type=jnp.float32))
        return (total + jnp.concatenate(head_outputs, axis=1), None)

    def one_shard(total, inputs):
        keys_s, values_s, bias_s, live_s = inputs
        start_share = jnp.zeros((CANDS, D), jnp.float32)
        share, unused_inner = lax.scan(one_user, start_share, (keys_s, values_s, bias_s, live_s, user_ids))
        rounded = lax.optimization_barrier(share.astype(jnp.bfloat16))
        return (total + rounded.astype(jnp.float32), None)
    start_total = jnp.zeros((CANDS, D), jnp.float32)
    attended, unused = lax.scan(one_shard, start_total, (shard_keys, shard_values, shard_bias, shard_live))
    row_mean = lax.optimization_barrier(jnp.sum(attended, axis=1)) / D
    row_var = lax.optimization_barrier(jnp.sum(attended * attended, axis=1)) / D - row_mean * row_mean
    cand_states = ((attended - row_mean[:, None]) * lax.rsqrt(row_var[:, None] + 1e-05) * cand_gate.astype(jnp.float32)).astype(jnp.bfloat16)
    pre_act = jnp.dot(cand_states, tower_in, preferred_element_type=jnp.float32) + tower_bias[None, :]
    hidden = jax.nn.silu(pre_act)
    cand_scores = jnp.dot(hidden, tower_out, precision=lax.Precision.HIGHEST)
    return (cand_states, cand_scores)
```

```python
import functools

import jax
import jax.numpy as jnp
from jax import lax
from jax.experimental import pallas as pl
from jax.experimental.pallas import tpu as pltpu
from jax.sharding import PartitionSpec as P

DH = 128
MESH = pl.DeviceIdType.MESH
F32 = jnp.float32
BF16 = jnp.bfloat16


def partner_of(me, step, count):
    if count & (count - 1):
        return lax.rem(me + step, count)
    other, bit = 0, 1
    while bit < count:
        mine = lax.rem(me // bit, 2)
        other = other + (1 - mine if step & bit else mine) * bit
        bit *= 2
    return other


def source_of(me, step, count):
    if count & (count - 1):
        return lax.rem(me + count - step, count)
    return partner_of(me, step, count)


def kernel(
    n_hist,
    n_tower,
    q_hbm,
    k_hbm,
    v_hbm,
    user_hbm,
    bucket_hbm,
    len_ref,
    gate_hbm,
    tbias_hbm,
    w_hbm,
    b_hbm,
    o_hbm,
    states_out,
    scores_out,
    q_all,
    u_all,
    k_buf,
    v_buf,
    bucket,
    gate,
    tbias,
    w_buf,
    b_buf,
    o_buf,
    share_out,
    share_in,
    stat_buf,
    state_buf,
    score_send,
    score_in,
    load_sem,
    q_send,
    q_recv,
    u_send,
    u_recv,
    share_send,
    share_recv,
    one_send,
    one_recv,
    state_send,
    state_recv,
    score_send_sem,
    score_recv,
):
    z = lax.axis_index("hist")
    x = lax.axis_index("tower")
    c = lax.axis_index("head")
    mate = 1 - c
    rows, feat = q_hbm.shape
    users, per_user, _ = k_hbm.shape
    hidden = b_buf.shape[1]
    total_feat = 2 * feat

    tower_peers = [(t, h) for t in range(n_tower) for h in range(2) if t or h]

    def tower_id(t, h):
        return {"tower": partner_of(x, t, n_tower), "head": mate if h else c}

    barrier = pltpu.get_barrier_semaphore()
    for step in range(1, n_hist):
        pl.semaphore_signal(
            barrier, inc=1, device_id={"hist": partner_of(z, step, n_hist)}, device_id_type=MESH
        )
    for t, h in tower_peers:
        pl.semaphore_signal(barrier, inc=1, device_id=tower_id(t, h), device_id_type=MESH)

    mine_cols = pl.ds(pl.multiple_of(c * hidden, 128), hidden)
    mate_cols = pl.ds(pl.multiple_of(mate * hidden, 128), hidden)
    loads = [
        pltpu.make_async_copy(src, dst, load_sem.at[i])
        for i, (src, dst) in enumerate(
            [
                (q_hbm, q_all.at[z]),
                (user_hbm, u_all.at[z]),
                (bucket_hbm, bucket),
                (tbias_hbm, tbias),
                (k_hbm, k_buf),
                (v_hbm, v_buf),
                (gate_hbm, gate),
                (b_hbm.at[:, mine_cols], b_buf),
                (o_hbm.at[:, mine_cols], o_buf),
                (w_hbm.at[:, mine_cols], w_buf.at[c]),
            ]
        )
    ]
    for load in loads:
        load.start()

    pl.semaphore_wait(barrier, n_hist - 1 + len(tower_peers))

    def remote(src, dst, send, recv, device_id):
        return pltpu.make_async_remote_copy(
            src_ref=src,
            dst_ref=dst,
            send_sem=send,
            recv_sem=recv,
            device_id=device_id,
            device_id_type=MESH,
        )

    sends = []
    order = list(range(2, n_hist)) + [1] if n_hist > 1 else []
    for step in order:
        to = {"hist": partner_of(z, step, n_hist)}
        u_copy = remote(user_hbm, u_all.at[z], u_send.at[step], u_recv.at[z], to)
        u_copy.start()
        q_copy = remote(q_hbm, q_all.at[z], q_send.at[step], q_recv.at[z], to)
        q_copy.start()
        sends += [u_copy, q_copy]
    w_copy = remote(
        w_hbm.at[:, mate_cols], w_buf.at[c], one_send.at[0], one_recv.at[0], {"head": mate}
    )
    w_copy.start()
    sends.append(w_copy)

    loads[2].wait()
    loads[3].wait()
    bucket_count, heads = tbias.shape
    half_scale = 0.5 * DH ** (-0.5)
    tb = tbias[...] * 0.5
    bias_rows, owner_rows = [], []
    for u in range(users):
        onehot = jnp.where(
            lax.broadcasted_iota(jnp.int32, (bucket_count, per_user), 0) == bucket[u : u + 1, :],
            1.0,
            0.0,
        ).astype(F32)
        bias_rows.append(
            lax.dot_general(
                tb,
                onehot,
                (((0,), (0,)), ((), ())),
                precision=lax.Precision.HIGHEST,
                preferred_element_type=F32,
            )
        )
        position = z * per_user + lax.broadcasted_iota(jnp.int32, (1, per_user), 1)
        owner_rows.append(jnp.where(position < len_ref[u], u, -1))
    bias = jnp.concatenate(bias_rows, axis=1)
    owner = jnp.concatenate(owner_rows, axis=1)
    events = users * per_user

    loads[0].wait()
    loads[1].wait()
    loads[4].wait()
    loads[5].wait()

    def attend(index, out_ref):
        user_col = jnp.broadcast_to(u_all[index], (128, rows)).T[:, :1]
        live = jnp.where(user_col == owner, 1.0, 0.0).astype(F32)
        for head in range(heads):
            cols = slice(head * DH, (head + 1) * DH)
            s = lax.dot_general(
                q_all[index, :, cols],
                k_buf[:, :, cols].reshape(events, DH),
                (((1,), (1,)), ((), ())),
                preferred_element_type=F32,
            )
            half = s * half_scale + bias[head : head + 1, :]
            weight = ((half + half * jnp.tanh(half)) * live).astype(BF16)
            out_ref[:, cols] = jnp.dot(
                weight, v_buf[:, :, cols].reshape(events, DH), preferred_element_type=F32
            ).astype(BF16)

    attend(z, share_in.at[z])
    for step in range(1, n_hist):
        src = source_of(z, step, n_hist)
        remote(user_hbm, u_all.at[src], u_send.at[step], u_recv.at[src], {"hist": src}).wait_recv()
        remote(q_hbm, q_all.at[src], q_send.at[step], q_recv.at[src], {"hist": src}).wait_recv()
        attend(src, share_out.at[step])
        copy = remote(
            share_out.at[step],
            share_in.at[z],
            share_send.at[step],
            share_recv.at[z],
            {"hist": src},
        )
        copy.start()
        sends.append(copy)

    for step in range(1, n_hist):
        src = partner_of(z, step, n_hist)
        remote(
            share_out.at[step], share_in.at[src], share_send.at[step], share_recv.at[src], {"hist": src}
        ).wait_recv()
    attended = share_in[0].astype(F32)
    for s in range(1, n_hist):
        attended = attended + share_in[s].astype(F32)

    row_sum = jnp.sum(attended, axis=1, keepdims=True)
    row_squares = jnp.sum(attended * attended, axis=1, keepdims=True)
    lane = lax.broadcasted_iota(jnp.int32, (rows, 128), 1)
    stat_buf[c] = jnp.where(lane == 0, row_sum, row_squares)
    stat_copy = remote(
        stat_buf.at[c], stat_buf.at[c], one_send.at[1], one_recv.at[1], {"head": mate}
    )
    stat_copy.start()
    sends.append(stat_copy)
    loads[6].wait()
    remote(
        stat_buf.at[mate], stat_buf.at[mate], one_send.at[1], one_recv.at[1], {"head": mate}
    ).wait_recv()
    stats = stat_buf[0] + stat_buf[1]
    row_mean = stats[:, 0:1] / total_feat
    row_var = stats[:, 1:2] / total_feat - row_mean * row_mean
    state_buf[x, c] = (
        (attended - row_mean) * lax.rsqrt(row_var + 1e-05) * gate[...].astype(F32)
    ).astype(BF16)

    for i, (t, h) in enumerate(tower_peers):
        copy = remote(
            state_buf.at[x, c],
            state_buf.at[x, c],
            state_send.at[i],
            state_recv.at[x, c],
            tower_id(t, h),
        )
        copy.start()
        sends.append(copy)
    states_out[...] = state_buf[x, c]

    loads[7].wait()
    loads[8].wait()
    loads[9].wait()
    remote(
        w_hbm.at[:, mate_cols], w_buf.at[mate], one_send.at[0], one_recv.at[0], {"head": mate}
    ).wait_recv()

    def wait_state(tower, head):
        remote(
            state_buf.at[tower, head],
            state_buf.at[tower, head],
            state_send.at[0],
            state_recv.at[tower, head],
            {"head": mate},
        ).wait_recv()

    def tower_scores(tower):
        pre = jnp.dot(state_buf[tower, 0], w_buf[0], preferred_element_type=F32)
        pre = pre + jnp.dot(state_buf[tower, 1], w_buf[1], preferred_element_type=F32)
        half = (pre + b_buf[...]) * 0.5
        part = (half + half * jnp.tanh(half)) * o_buf[...]
        acc = part[:, 0:128]
        for i in range(1, hidden // 128):
            acc = acc + part[:, i * 128 : (i + 1) * 128]
        return jnp.broadcast_to(jnp.sum(acc.T, axis=0, keepdims=True), (8, rows))

    wait_state(x, mate)
    own_scores = tower_scores(x)
    score_in[x, c] = own_scores
    copy = remote(
        score_in.at[x, c], score_in.at[x, c], score_send_sem.at[0], score_recv.at[x, c], {"head": mate}
    )
    copy.start()
    sends.append(copy)
    for t in range(1, n_tower):
        other = source_of(x, t, n_tower)
        wait_state(other, c)
        wait_state(other, mate)
        score_send[t] = tower_scores(other)
        for h in range(2):
            copy = remote(
                score_send.at[t],
                score_in.at[x, c],
                score_send_sem.at[2 * t + h],
                score_recv.at[x, c],
                {"tower": other, "head": mate if h else c},
            )
            copy.start()
            sends.append(copy)

    for t, h in tower_peers:
        tower, head = partner_of(x, t, n_tower), mate if h else c
        remote(
            score_in.at[tower, head],
            score_in.at[tower, head],
            score_send_sem.at[0],
            score_recv.at[tower, head],
            {"head": mate},
        ).wait_recv()
    total = score_in[0, 0] + score_in[0, 1]
    for t in range(1, n_tower):
        total = total + (score_in[t, 0] + score_in[t, 1])
    scores_out[...] = total[0:1, :]
    for copy in sends:
        copy.wait_send()


def local(
    queries,
    hist_keys,
    hist_values,
    cand_user,
    time_bucket,
    hist_len,
    cand_gate,
    time_bias,
    tower_in,
    tower_bias,
    tower_out,
    *,
    n_hist,
    n_tower,
):
    rows, feat = queries.shape
    hidden = tower_in.shape[1] // 2
    any_spec = pl.BlockSpec(memory_space=pl.ANY)
    vmem_spec = pl.BlockSpec(memory_space=pltpu.VMEM)
    dma = pltpu.SemaphoreType.DMA
    states, scores = pl.pallas_call(
        functools.partial(kernel, n_hist, n_tower),
        out_shape=(
            jax.ShapeDtypeStruct((rows, feat), BF16),
            jax.ShapeDtypeStruct((1, rows), F32),
        ),
        in_specs=[any_spec] * 5 + [pl.BlockSpec(memory_space=pltpu.SMEM)] + [any_spec] * 5,
        out_specs=(vmem_spec, vmem_spec),
        scratch_shapes=[
            pltpu.VMEM((n_hist, rows, feat), BF16),
            pltpu.VMEM((n_hist, 1, rows), jnp.int32),
            pltpu.VMEM(hist_keys.shape, BF16),
            pltpu.VMEM(hist_values.shape, BF16),
            pltpu.VMEM(time_bucket.shape, jnp.int32),
            pltpu.VMEM((rows, feat), BF16),
            pltpu.VMEM(time_bias.shape, F32),
            pltpu.VMEM((2, feat, hidden), BF16),
            pltpu.VMEM((1, hidden), F32),
            pltpu.VMEM((1, hidden), F32),
            pltpu.VMEM((n_hist, rows, feat), BF16),
            pltpu.VMEM((n_hist, rows, feat), BF16),
            pltpu.VMEM((2, rows, 128), F32),
            pltpu.VMEM((n_tower, 2, rows, feat), BF16),
            pltpu.VMEM((n_tower, 8, rows), F32),
            pltpu.VMEM((n_tower, 2, 8, rows), F32),
            dma((10,)),
            dma((n_hist,)),
            dma((n_hist,)),
            dma((n_hist,)),
            dma((n_hist,)),
            dma((n_hist,)),
            dma((n_hist,)),
            dma((2,)),
            dma((2,)),
            dma((2 * n_tower,)),
            dma((n_tower, 2)),
            dma((2 * n_tower,)),
            dma((n_tower, 2)),
        ],
        compiler_params=pltpu.CompilerParams(collective_id=0, has_side_effects=True),
    )(
        queries,
        hist_keys,
        hist_values,
        cand_user.reshape(1, rows),
        time_bucket,
        hist_len,
        cand_gate,
        time_bias,
        tower_in,
        tower_bias.reshape(1, -1),
        tower_out.reshape(1, -1),
    )
    return states, scores.reshape(rows)


def solution(mesh):
    return jax.shard_map(
        functools.partial(local, n_hist=mesh.shape["hist"], n_tower=mesh.shape["tower"]),
        mesh=mesh,
        in_specs=(
            P(("groups", "hist", "tower"), "head"),
            P("groups", "hist", "head"),
            P("groups", "hist", "head"),
            P(("groups", "hist", "tower")),
            P("groups", "hist"),
            P("groups"),
            P(("groups", "hist", "tower"), "head"),
            P(None, "head"),
            P("head", "tower"),
            P("tower"),
            P("tower"),
        ),
        out_specs=(P(("groups", "hist", "tower"), "head"), P(("groups", "hist", "tower"))),
        check_vma=False,
    )
```

```python
import functools

import jax
import jax.numpy as jnp
from jax import lax
from jax.experimental import pallas as pl
from jax.experimental.pallas import tpu as pltpu
from jax.sharding import PartitionSpec as P

DH = 128
CHUNKS = 2
MESH = pl.DeviceIdType.MESH
F32 = jnp.float32
BF16 = jnp.bfloat16


def partner_of(me, step, count):
    if count & (count - 1):
        return lax.rem(me + step, count)
    other, bit = 0, 1
    while bit < count:
        mine = lax.rem(me // bit, 2)
        other = other + (1 - mine if step & bit else mine) * bit
        bit *= 2
    return other


def source_of(me, step, count):
    if count & (count - 1):
        return lax.rem(me + count - step, count)
    return partner_of(me, step, count)


def kernel(
    n_hist,
    n_tower,
    q_hbm,
    k_hbm,
    v_hbm,
    user_hbm,
    bucket_hbm,
    len_ref,
    gate_hbm,
    tbias_hbm,
    w_hbm,
    b_hbm,
    o_hbm,
    states_out,
    scores_out,
    q_own,
    q_all,
    u_all,
    k_buf,
    v_buf,
    bucket,
    gate,
    tbias,
    w_buf,
    b_buf,
    o_buf,
    share_out,
    share_in,
    stat_buf,
    state_buf,
    score_send,
    score_in,
    load_sem,
    ready,
    q_send,
    q_recv,
    u_send,
    u_recv,
    share_send,
    share_recv,
    one_send,
    one_recv,
    state_send,
    state_recv,
    score_send_sem,
    score_recv,
):
    z = lax.axis_index("hist")
    x = lax.axis_index("tower")
    c = lax.axis_index("head")
    mate = 1 - c
    rows, feat = q_hbm.shape
    users, per_user, _ = k_hbm.shape
    hidden = b_buf.shape[1]
    total_feat = 2 * feat

    tower_peers = [(t, h) for t in range(n_tower) for h in range(2) if t or h]

    def tower_id(t, h):
        return {"tower": partner_of(x, t, n_tower), "head": mate if h else c}

    has_left, has_right = z > 0, z < n_hist - 1
    sides = ((has_left, z - 1), (has_right, z + 1))

    barrier = pltpu.get_barrier_semaphore()
    for exists, there in sides:

        @pl.when(exists)
        def _(there=there):
            pl.semaphore_signal(barrier, inc=1, device_id={"hist": there}, device_id_type=MESH)

    for t, h in tower_peers:
        pl.semaphore_signal(barrier, inc=1, device_id=tower_id(t, h), device_id_type=MESH)

    mine_cols = pl.ds(pl.multiple_of(c * hidden, 128), hidden)
    mate_cols = pl.ds(pl.multiple_of(mate * hidden, 128), hidden)
    loads = [
        pltpu.make_async_copy(src, dst, load_sem.at[i])
        for i, (src, dst) in enumerate(
            [
                (q_hbm, q_own),
                (user_hbm, u_all.at[z]),
                (bucket_hbm, bucket),
                (tbias_hbm, tbias),
                (k_hbm, k_buf),
                (v_hbm, v_buf),
                (gate_hbm, gate),
                (b_hbm.at[:, mine_cols], b_buf),
                (o_hbm.at[:, mine_cols], o_buf),
                (w_hbm.at[:, mine_cols], w_buf.at[c]),
            ]
        )
    ]
    for load in loads:
        load.start()

    neighbours = has_left.astype(jnp.int32) + has_right.astype(jnp.int32)
    pl.semaphore_wait(barrier, neighbours + len(tower_peers))

    def remote(src, dst, send, recv, device_id):
        return pltpu.make_async_remote_copy(
            src_ref=src,
            dst_ref=dst,
            send_sem=send,
            recv_sem=recv,
            device_id=device_id,
            device_id_type=MESH,
        )

    chunks = q_all.shape[1]
    width = feat // chunks

    def query_copy(there, chunk):
        return remote(
            q_hbm.at[:, chunk * width : (chunk + 1) * width],
            q_all.at[z, chunk],
            q_send.at[there, chunk],
            q_recv.at[z, chunk],
            {"hist": there},
        )

    def user_copy(there):
        return remote(user_hbm, u_all.at[z], u_send.at[there], u_recv.at[z], {"hist": there})

    def each_other(action):
        for distance in range(1, n_hist):
            for sign, behind in ((-1, has_right), (1, has_left)):
                there = z + sign * distance
                pl.when((there >= 0) & (there < n_hist))(
                    functools.partial(action, distance, there, z - sign, behind)
                )

    def send_queries(distance, there, back, behind):
        if distance > 1:
            pl.semaphore_wait(ready.at[there], 1)

        @pl.when(behind)
        def _():
            pl.semaphore_signal(
                ready.at[there], inc=1, device_id={"hist": back}, device_id_type=MESH
            )

        user_copy(there).start()
        for chunk in range(chunks):
            query_copy(there, chunk).start()

    each_other(send_queries)
    sends = []
    w_copy = remote(
        w_hbm.at[:, mate_cols], w_buf.at[c], one_send.at[0], one_recv.at[0], {"head": mate}
    )
    w_copy.start()
    sends.append(w_copy)

    loads[2].wait()
    loads[3].wait()
    heads, bucket_count = tbias.shape
    half_scale = 0.5 * DH ** (-0.5)
    tb = tbias[...] * 0.5
    bias_rows, owner_rows = [], []
    for u in range(users):
        onehot = jnp.where(
            lax.broadcasted_iota(jnp.int32, (bucket_count, per_user), 0) == bucket[u : u + 1, :],
            1.0,
            0.0,
        ).astype(F32)
        bias_rows.append(
            lax.dot_general(
                tb,
                onehot,
                (((1,), (0,)), ((), ())),
                precision=lax.Precision.HIGHEST,
                preferred_element_type=F32,
            )
        )
        position = z * per_user + lax.broadcasted_iota(jnp.int32, (1, per_user), 1)
        owner_rows.append(jnp.where(position < len_ref[u], u, -1))
    bias = jnp.concatenate(bias_rows, axis=1)
    owner = jnp.concatenate(owner_rows, axis=1)
    events = users * per_user

    loads[0].wait()
    loads[1].wait()
    loads[4].wait()
    loads[5].wait()

    def live_of(index):
        user_col = jnp.broadcast_to(u_all[index], (128, rows)).T[:, :1]
        return jnp.where(user_col == owner, 1.0, 0.0).astype(F32)

    def attend(query, live, head):
        cols = slice(head * DH, (head + 1) * DH)
        s = lax.dot_general(
            query,
            k_buf[:, :, cols].reshape(events, DH),
            (((1,), (1,)), ((), ())),
            preferred_element_type=F32,
        )
        half = s * half_scale + bias[head : head + 1, :]
        weight = ((half + half * jnp.tanh(half)) * live).astype(BF16)
        return jnp.dot(
            weight, v_buf[:, :, cols].reshape(events, DH), preferred_element_type=F32
        ).astype(BF16)

    per_chunk = heads // chunks
    own_live = live_of(z)
    for head in range(heads):
        cols = slice((head % per_chunk) * DH, (head % per_chunk + 1) * DH)
        share_in[z, head // per_chunk, :, cols] = attend(
            q_own[:, head * DH : (head + 1) * DH], own_live, head
        )

    nearer = jnp.minimum(z, n_hist - 1 - z)

    def block_at(step):
        distance = (step + 1) // 2
        paired = z - distance if step % 2 else z + distance
        rest = jnp.where(z < n_hist - 1 - z, z + step - nearer, z - step + nearer)
        return jnp.where(step <= 2 * nearer, paired, rest)

    def arrive(block, chunk):
        if chunk == 0:
            remote(
                user_hbm, u_all.at[block], u_send.at[block], u_recv.at[block], {"hist": block}
            ).wait_recv()
        remote(
            q_hbm.at[:, 0:width],
            q_all.at[block, chunk],
            q_send.at[block, chunk],
            q_recv.at[block, chunk],
            {"hist": block},
        ).wait_recv()

    def share_copy(step, chunk):
        return remote(
            share_out.at[step, chunk],
            share_in.at[z, chunk],
            share_send.at[step, chunk],
            share_recv.at[z, chunk],
            {"hist": block_at(step)},
        )

    for step in range(1, n_hist):
        block = block_at(step)
        for chunk in range(chunks):
            arrive(block, chunk)
            if chunk == 0:
                live = live_of(block)
            for i in range(per_chunk):
                cols = slice(i * DH, (i + 1) * DH)
                share_out[step, chunk, :, cols] = attend(
                    q_all[block, chunk, :, cols], live, chunk * per_chunk + i
                )
            copy = share_copy(step, chunk)
            copy.start()
            sends.append(copy)

    for step in range(1, n_hist):
        src = block_at(step)
        for chunk in range(chunks):
            remote(
                share_out.at[step, chunk],
                share_in.at[src, chunk],
                share_send.at[step, chunk],
                share_recv.at[src, chunk],
                {"hist": src},
            ).wait_recv()
    parts = []
    for chunk in range(chunks):
        part = share_in[0, chunk].astype(F32)
        for s in range(1, n_hist):
            part = part + share_in[s, chunk].astype(F32)
        parts.append(part)
    attended = jnp.concatenate(parts, axis=1)

    row_sum = jnp.sum(attended, axis=1, keepdims=True)
    row_squares = jnp.sum(attended * attended, axis=1, keepdims=True)
    lane = lax.broadcasted_iota(jnp.int32, (rows, 128), 1)
    stat_buf[c] = jnp.where(lane == 0, row_sum, row_squares)
    stat_copy = remote(
        stat_buf.at[c], stat_buf.at[c], one_send.at[1], one_recv.at[1], {"head": mate}
    )
    stat_copy.start()
    sends.append(stat_copy)
    loads[6].wait()
    remote(
        stat_buf.at[mate], stat_buf.at[mate], one_send.at[1], one_recv.at[1], {"head": mate}
    ).wait_recv()
    stats = stat_buf[0] + stat_buf[1]
    row_mean = stats[:, 0:1] / total_feat
    row_var = stats[:, 1:2] / total_feat - row_mean * row_mean
    state_buf[x, c] = (
        (attended - row_mean) * lax.rsqrt(row_var + 1e-05) * gate[...].astype(F32)
    ).astype(BF16)

    for i, (t, h) in enumerate(tower_peers):
        copy = remote(
            state_buf.at[x, c],
            state_buf.at[x, c],
            state_send.at[i],
            state_recv.at[x, c],
            tower_id(t, h),
        )
        copy.start()
        sends.append(copy)
    states_out[...] = state_buf[x, c]

    loads[7].wait()
    loads[8].wait()
    loads[9].wait()
    remote(
        w_hbm.at[:, mate_cols], w_buf.at[mate], one_send.at[0], one_recv.at[0], {"head": mate}
    ).wait_recv()

    def wait_state(tower, head):
        remote(
            state_buf.at[tower, head],
            state_buf.at[tower, head],
            state_send.at[0],
            state_recv.at[tower, head],
            {"head": mate},
        ).wait_recv()

    def tower_scores(tower):
        pre = jnp.dot(state_buf[tower, 0], w_buf[0], preferred_element_type=F32)
        pre = pre + jnp.dot(state_buf[tower, 1], w_buf[1], preferred_element_type=F32)
        half = (pre + b_buf[...]) * 0.5
        part = (half + half * jnp.tanh(half)) * o_buf[...]
        acc = part[:, 0:128]
        for i in range(1, hidden // 128):
            acc = acc + part[:, i * 128 : (i + 1) * 128]
        return jnp.broadcast_to(jnp.sum(acc.T, axis=0, keepdims=True), (8, rows))

    wait_state(x, mate)
    own_scores = tower_scores(x)
    score_in[x, c] = own_scores
    copy = remote(
        score_in.at[x, c], score_in.at[x, c], score_send_sem.at[0], score_recv.at[x, c], {"head": mate}
    )
    copy.start()
    sends.append(copy)
    for t in range(1, n_tower):
        other = source_of(x, t, n_tower)
        wait_state(other, c)
        wait_state(other, mate)
        score_send[t] = tower_scores(other)
        for h in range(2):
            copy = remote(
                score_send.at[t],
                score_in.at[x, c],
                score_send_sem.at[2 * t + h],
                score_recv.at[x, c],
                {"tower": other, "head": mate if h else c},
            )
            copy.start()
            sends.append(copy)

    for t, h in tower_peers:
        tower, head = partner_of(x, t, n_tower), mate if h else c
        remote(
            score_in.at[tower, head],
            score_in.at[tower, head],
            score_send_sem.at[0],
            score_recv.at[tower, head],
            {"head": mate},
        ).wait_recv()
    total = score_in[0, 0] + score_in[0, 1]
    for t in range(1, n_tower):
        total = total + (score_in[t, 0] + score_in[t, 1])
    scores_out[...] = total[0:1, :]
    for copy in sends:
        copy.wait_send()

    def sent(distance, there, back, behind):
        user_copy(there).wait_send()
        for chunk in range(chunks):
            query_copy(there, chunk).wait_send()

    each_other(sent)


def hand_over(states_in, scores_in, states_out, scores_out):
    states_out[...] = states_in[...]
    scores_out[...] = scores_in[...]


def local(
    queries,
    hist_keys,
    hist_values,
    cand_user,
    time_bucket,
    hist_len,
    cand_gate,
    time_bias,
    tower_in,
    tower_bias,
    tower_out,
    *,
    n_hist,
    n_tower,
):
    rows, feat = queries.shape
    hidden = tower_in.shape[1] // 2
    chunks = CHUNKS if (feat // DH) % CHUNKS == 0 else 1
    any_spec = pl.BlockSpec(memory_space=pl.ANY)
    vmem_spec = pl.BlockSpec(memory_space=pltpu.VMEM)
    dma = pltpu.SemaphoreType.DMA
    states, scores = pl.pallas_call(
        functools.partial(kernel, n_hist, n_tower),
        out_shape=(
            jax.ShapeDtypeStruct((rows, feat), BF16),
            jax.ShapeDtypeStruct((1, rows), F32),
        ),
        in_specs=[any_spec] * 5 + [pl.BlockSpec(memory_space=pltpu.SMEM)] + [any_spec] * 5,
        out_specs=(vmem_spec, vmem_spec),
        scratch_shapes=[
            pltpu.VMEM((rows, feat), BF16),
            pltpu.VMEM((n_hist, chunks, rows, feat // chunks), BF16),
            pltpu.VMEM((n_hist, 1, rows), jnp.int32),
            pltpu.VMEM(hist_keys.shape, BF16),
            pltpu.VMEM(hist_values.shape, BF16),
            pltpu.VMEM(time_bucket.shape, jnp.int32),
            pltpu.VMEM((rows, feat), BF16),
            pltpu.VMEM(time_bias.shape[::-1], F32),
            pltpu.VMEM((2, feat, hidden), BF16),
            pltpu.VMEM((1, hidden), F32),
            pltpu.VMEM((1, hidden), F32),
            pltpu.VMEM((n_hist, chunks, rows, feat // chunks), BF16),
            pltpu.VMEM((n_hist, chunks, rows, feat // chunks), BF16),
            pltpu.VMEM((2, rows, 128), F32),
            pltpu.VMEM((n_tower, 2, rows, feat), BF16),
            pltpu.VMEM((n_tower, 8, rows), F32),
            pltpu.VMEM((n_tower, 2, 8, rows), F32),
            dma((10,)),
            pltpu.SemaphoreType.REGULAR((n_hist,)),
            dma((n_hist, chunks)),
            dma((n_hist, chunks)),
            dma((n_hist,)),
            dma((n_hist,)),
            dma((n_hist, chunks)),
            dma((n_hist, chunks)),
            dma((2,)),
            dma((2,)),
            dma((2 * n_tower,)),
            dma((n_tower, 2)),
            dma((2 * n_tower,)),
            dma((n_tower, 2)),
        ],
        compiler_params=pltpu.CompilerParams(collective_id=0, has_side_effects=True),
    )(
        queries,
        hist_keys,
        hist_values,
        cand_user.reshape(1, rows),
        time_bucket,
        hist_len,
        cand_gate,
        time_bias.T,
        tower_in,
        tower_bias.reshape(1, -1),
        tower_out.reshape(1, -1),
    )
    states, scores = pl.pallas_call(
        hand_over,
        out_shape=(
            jax.ShapeDtypeStruct((rows, feat), BF16),
            jax.ShapeDtypeStruct((1, rows), F32),
        ),
        in_specs=[vmem_spec, vmem_spec],
        out_specs=(vmem_spec, vmem_spec),
    )(states, scores)
    return states, scores.reshape(rows)


def solution(mesh):
    return jax.shard_map(
        functools.partial(local, n_hist=mesh.shape["hist"], n_tower=mesh.shape["tower"]),
        mesh=mesh,
        in_specs=(
            P(("groups", "hist", "tower"), "head"),
            P("groups", "hist", "head"),
            P("groups", "hist", "head"),
            P(("groups", "hist", "tower")),
            P("groups", "hist"),
            P("groups"),
            P(("groups", "hist", "tower"), "head"),
            P(None, "head"),
            P("head", "tower"),
            P("tower"),
            P("tower"),
        ),
        out_specs=(P(("groups", "hist", "tower"), "head"), P(("groups", "hist", "tower"))),
        check_vma=False,
    )
```

```python
import functools

import jax
import jax.numpy as jnp
from jax import lax
from jax.experimental import pallas as pl
from jax.experimental.pallas import tpu as pltpu
from jax.sharding import PartitionSpec as P

DH = 128
CHUNKS = 2
MESH = pl.DeviceIdType.MESH
F32 = jnp.float32
BF16 = jnp.bfloat16


def partner_of(me, step, count):
    if count & (count - 1):
        return lax.rem(me + step, count)
    other, bit = 0, 1
    while bit < count:
        mine = lax.rem(me // bit, 2)
        other = other + (1 - mine if step & bit else mine) * bit
        bit *= 2
    return other


def source_of(me, step, count):
    if count & (count - 1):
        return lax.rem(me + count - step, count)
    return partner_of(me, step, count)


def kernel(
    n_hist,
    n_tower,
    q_hbm,
    k_hbm,
    v_hbm,
    user_hbm,
    bucket_hbm,
    len_ref,
    gate_hbm,
    tbias_hbm,
    w_hbm,
    b_hbm,
    o_hbm,
    states_out,
    scores_out,
    q_own,
    q_all,
    u_all,
    k_buf,
    v_buf,
    bucket,
    gate,
    tbias,
    w_buf,
    b_buf,
    o_buf,
    share_out,
    share_in,
    stat_buf,
    state_buf,
    score_send,
    score_in,
    load_sem,
    ready,
    pass_send,
    q_send,
    q_recv,
    u_send,
    u_recv,
    share_send,
    share_recv,
    one_send,
    one_recv,
    state_send,
    state_recv,
    score_send_sem,
    score_recv,
):
    z = lax.axis_index("hist")
    x = lax.axis_index("tower")
    c = lax.axis_index("head")
    mate = 1 - c
    rows, feat = q_hbm.shape
    users, per_user, _ = k_hbm.shape
    hidden = b_buf.shape[1]
    total_feat = 2 * feat

    tower_peers = [(t, h) for t in range(n_tower) for h in range(2) if t or h]

    def tower_id(t, h):
        return {"tower": partner_of(x, t, n_tower), "head": mate if h else c}

    has_left, has_right = z > 0, z < n_hist - 1
    sides = ((has_left, z - 1), (has_right, z + 1))

    barrier = pltpu.get_barrier_semaphore()
    for exists, there in sides:

        @pl.when(exists)
        def _(there=there):
            pl.semaphore_signal(barrier, inc=1, device_id={"hist": there}, device_id_type=MESH)

    for t, h in tower_peers:
        pl.semaphore_signal(barrier, inc=1, device_id=tower_id(t, h), device_id_type=MESH)

    mine_cols = pl.ds(pl.multiple_of(c * hidden, 128), hidden)
    mate_cols = pl.ds(pl.multiple_of(mate * hidden, 128), hidden)
    loads = [
        pltpu.make_async_copy(src, dst, load_sem.at[i])
        for i, (src, dst) in enumerate(
            [
                (q_hbm, q_own),
                (user_hbm, u_all.at[z]),
                (bucket_hbm, bucket),
                (tbias_hbm, tbias),
                (k_hbm, k_buf),
                (v_hbm, v_buf),
                (gate_hbm, gate),
                (b_hbm.at[:, mine_cols], b_buf),
                (o_hbm.at[:, mine_cols], o_buf),
                (w_hbm.at[:, mine_cols], w_buf.at[c]),
            ]
        )
    ]
    for load in loads:
        load.start()

    neighbours = has_left.astype(jnp.int32) + has_right.astype(jnp.int32)
    pl.semaphore_wait(barrier, neighbours + len(tower_peers))

    def remote(src, dst, send, recv, device_id):
        return pltpu.make_async_remote_copy(
            src_ref=src,
            dst_ref=dst,
            send_sem=send,
            recv_sem=recv,
            device_id=device_id,
            device_id_type=MESH,
        )

    chunks = q_all.shape[1]
    width = feat // chunks

    def query_copy(there, chunk):
        return remote(
            q_hbm.at[:, chunk * width : (chunk + 1) * width],
            q_all.at[z, chunk],
            q_send.at[there, chunk],
            q_recv.at[z, chunk],
            {"hist": there},
        )

    def user_copy(there):
        return remote(user_hbm, u_all.at[z], u_send.at[there], u_recv.at[z], {"hist": there})

    def each_other(action):
        for distance in range(1, n_hist):
            for sign, behind in ((-1, has_right), (1, has_left)):
                there = z + sign * distance
                pl.when((there >= 0) & (there < n_hist))(
                    functools.partial(action, distance, there, z - sign, behind)
                )

    def goes_direct(distance, behind):
        return jnp.logical_not(behind) if distance == 2 else z >= 0

    passes = (
        ((z >= 2) & (z + 1 < n_hist), z - 1, z + 1),
        ((z >= 1) & (z + 2 < n_hist), z + 1, z - 1),
    )

    def pass_copy(way, block, there, chunk):
        return remote(
            q_all.at[block, chunk],
            q_all.at[block, chunk],
            pass_send.at[way, chunk],
            q_recv.at[block, chunk],
            {"hist": there},
        )

    def send_queries(distance, there, back, behind):
        if distance > 1:
            pl.semaphore_wait(ready.at[there], 1)

        @pl.when(behind)
        def _():
            pl.semaphore_signal(
                ready.at[there], inc=1, device_id={"hist": back}, device_id_type=MESH
            )

        user_copy(there).start()

        @pl.when(goes_direct(distance, behind))
        def _():
            for chunk in range(chunks):
                query_copy(there, chunk).start()

    each_other(send_queries)
    sends = []
    w_copy = remote(
        w_hbm.at[:, mate_cols], w_buf.at[c], one_send.at[0], one_recv.at[0], {"head": mate}
    )
    w_copy.start()
    sends.append(w_copy)

    loads[2].wait()
    loads[3].wait()
    heads, bucket_count = tbias.shape
    half_scale = 0.5 * DH ** (-0.5)
    tb = tbias[...] * 0.5
    bias_rows, owner_rows = [], []
    for u in range(users):
        onehot = jnp.where(
            lax.broadcasted_iota(jnp.int32, (bucket_count, per_user), 0) == bucket[u : u + 1, :],
            1.0,
            0.0,
        ).astype(F32)
        bias_rows.append(
            lax.dot_general(
                tb,
                onehot,
                (((1,), (0,)), ((), ())),
                precision=lax.Precision.HIGHEST,
                preferred_element_type=F32,
            )
        )
        position = z * per_user + lax.broadcasted_iota(jnp.int32, (1, per_user), 1)
        owner_rows.append(jnp.where(position < len_ref[u], u, -1))
    bias = jnp.concatenate(bias_rows, axis=1)
    owner = jnp.concatenate(owner_rows, axis=1)
    events = users * per_user

    loads[0].wait()
    loads[1].wait()
    loads[4].wait()
    loads[5].wait()

    def live_of(index):
        user_col = jnp.broadcast_to(u_all[index], (128, rows)).T[:, :1]
        return jnp.where(user_col == owner, 1.0, 0.0).astype(F32)

    def attend(query, live, head):
        cols = slice(head * DH, (head + 1) * DH)
        s = lax.dot_general(
            query,
            k_buf[:, :, cols].reshape(events, DH),
            (((1,), (1,)), ((), ())),
            preferred_element_type=F32,
        )
        half = s * half_scale + bias[head : head + 1, :]
        weight = ((half + half * jnp.tanh(half)) * live).astype(BF16)
        return jnp.dot(
            weight, v_buf[:, :, cols].reshape(events, DH), preferred_element_type=F32
        ).astype(BF16)

    per_chunk = heads // chunks
    own_live = live_of(z)
    for head in range(heads):
        cols = slice((head % per_chunk) * DH, (head % per_chunk + 1) * DH)
        share_in[z, head // per_chunk, :, cols] = attend(
            q_own[:, head * DH : (head + 1) * DH], own_live, head
        )

    nearer = jnp.minimum(z, n_hist - 1 - z)

    def block_at(step):
        distance = (step + 1) // 2
        paired = z - distance if step % 2 else z + distance
        rest = jnp.where(z < n_hist - 1 - z, z + step - nearer, z - step + nearer)
        return jnp.where(step <= 2 * nearer, paired, rest)

    def users_arrive(block):
        remote(
            user_hbm, u_all.at[block], u_send.at[block], u_recv.at[block], {"hist": block}
        ).wait_recv()

    def arrive(block, chunk):
        remote(
            q_hbm.at[:, 0:width],
            q_all.at[block, chunk],
            q_send.at[block, chunk],
            q_recv.at[block, chunk],
            {"hist": block},
        ).wait_recv()

    def share_copy(step, chunk):
        return remote(
            share_out.at[step, chunk],
            share_in.at[z, chunk],
            share_send.at[step, chunk],
            share_recv.at[z, chunk],
            {"hist": block_at(step)},
        )

    for chunk in range(chunks):
        for way, (passing, block, there) in enumerate(passes):

            @pl.when(passing)
            def _(way=way, block=block, there=there, chunk=chunk):
                arrive(block, chunk)
                pass_copy(way, block, there, chunk).start()

    for step in range(1, n_hist):
        block = block_at(step)
        taken = (passes[0][0] & (block == z - 1)) | (passes[1][0] & (block == z + 1))
        for chunk in range(chunks):
            if chunk == 0:
                users_arrive(block)

            @pl.when(jnp.logical_not(taken))
            def _(block=block, chunk=chunk):
                arrive(block, chunk)

            if chunk == 0:
                live = live_of(block)
            for i in range(per_chunk):
                cols = slice(i * DH, (i + 1) * DH)
                share_out[step, chunk, :, cols] = attend(
                    q_all[block, chunk, :, cols], live, chunk * per_chunk + i
                )
            copy = share_copy(step, chunk)
            copy.start()
            sends.append(copy)

    for step in range(1, n_hist):
        src = block_at(step)
        for chunk in range(chunks):
            remote(
                share_out.at[step, chunk],
                share_in.at[src, chunk],
                share_send.at[step, chunk],
                share_recv.at[src, chunk],
                {"hist": src},
            ).wait_recv()
    parts = []
    for chunk in range(chunks):
        part = share_in[0, chunk].astype(F32)
        for s in range(1, n_hist):
            part = part + share_in[s, chunk].astype(F32)
        parts.append(part)
    attended = jnp.concatenate(parts, axis=1)

    row_sum = jnp.sum(attended, axis=1, keepdims=True)
    row_squares = jnp.sum(attended * attended, axis=1, keepdims=True)
    lane = lax.broadcasted_iota(jnp.int32, (rows, 128), 1)
    stat_buf[c] = jnp.where(lane == 0, row_sum, row_squares)
    stat_copy = remote(
        stat_buf.at[c], stat_buf.at[c], one_send.at[1], one_recv.at[1], {"head": mate}
    )
    stat_copy.start()
    sends.append(stat_copy)
    loads[6].wait()
    remote(
        stat_buf.at[mate], stat_buf.at[mate], one_send.at[1], one_recv.at[1], {"head": mate}
    ).wait_recv()
    stats = stat_buf[0] + stat_buf[1]
    row_mean = stats[:, 0:1] / total_feat
    row_var = stats[:, 1:2] / total_feat - row_mean * row_mean
    state_buf[x, c] = (
        (attended - row_mean) * lax.rsqrt(row_var + 1e-05) * gate[...].astype(F32)
    ).astype(BF16)

    for i, (t, h) in enumerate(tower_peers):
        copy = remote(
            state_buf.at[x, c],
            state_buf.at[x, c],
            state_send.at[i],
            state_recv.at[x, c],
            tower_id(t, h),
        )
        copy.start()
        sends.append(copy)
    states_out[...] = state_buf[x, c]

    loads[7].wait()
    loads[8].wait()
    loads[9].wait()
    remote(
        w_hbm.at[:, mate_cols], w_buf.at[mate], one_send.at[0], one_recv.at[0], {"head": mate}
    ).wait_recv()

    def wait_state(tower, head):
        remote(
            state_buf.at[tower, head],
            state_buf.at[tower, head],
            state_send.at[0],
            state_recv.at[tower, head],
            {"head": mate},
        ).wait_recv()

    def tower_scores(tower):
        pre = jnp.dot(state_buf[tower, 0], w_buf[0], preferred_element_type=F32)
        pre = pre + jnp.dot(state_buf[tower, 1], w_buf[1], preferred_element_type=F32)
        half = (pre + b_buf[...]) * 0.5
        part = (half + half * jnp.tanh(half)) * o_buf[...]
        acc = part[:, 0:128]
        for i in range(1, hidden // 128):
            acc = acc + part[:, i * 128 : (i + 1) * 128]
        return jnp.broadcast_to(jnp.sum(acc.T, axis=0, keepdims=True), (8, rows))

    wait_state(x, mate)
    own_scores = tower_scores(x)
    score_in[x, c] = own_scores
    copy = remote(
        score_in.at[x, c], score_in.at[x, c], score_send_sem.at[0], score_recv.at[x, c], {"head": mate}
    )
    copy.start()
    sends.append(copy)
    for t in range(1, n_tower):
        other = source_of(x, t, n_tower)
        wait_state(other, c)
        wait_state(other, mate)
        score_send[t] = tower_scores(other)
        for h in range(2):
            copy = remote(
                score_send.at[t],
                score_in.at[x, c],
                score_send_sem.at[2 * t + h],
                score_recv.at[x, c],
                {"tower": other, "head": mate if h else c},
            )
            copy.start()
            sends.append(copy)

    for t, h in tower_peers:
        tower, head = partner_of(x, t, n_tower), mate if h else c
        remote(
            score_in.at[tower, head],
            score_in.at[tower, head],
            score_send_sem.at[0],
            score_recv.at[tower, head],
            {"head": mate},
        ).wait_recv()
    total = score_in[0, 0] + score_in[0, 1]
    for t in range(1, n_tower):
        total = total + (score_in[t, 0] + score_in[t, 1])
    scores_out[...] = total[0:1, :]
    for copy in sends:
        copy.wait_send()

    def sent(distance, there, back, behind):
        user_copy(there).wait_send()

        @pl.when(goes_direct(distance, behind))
        def _():
            for chunk in range(chunks):
                query_copy(there, chunk).wait_send()

    each_other(sent)
    for way, (passing, block, there) in enumerate(passes):

        @pl.when(passing)
        def _(way=way, block=block, there=there):
            for chunk in range(chunks):
                pass_copy(way, block, there, chunk).wait_send()


def hand_over(states_in, scores_in, states_out, scores_out):
    states_out[...] = states_in[...]
    scores_out[...] = scores_in[...]


def local(
    queries,
    hist_keys,
    hist_values,
    cand_user,
    time_bucket,
    hist_len,
    cand_gate,
    time_bias,
    tower_in,
    tower_bias,
    tower_out,
    *,
    n_hist,
    n_tower,
):
    rows, feat = queries.shape
    hidden = tower_in.shape[1] // 2
    chunks = CHUNKS if (feat // DH) % CHUNKS == 0 else 1
    any_spec = pl.BlockSpec(memory_space=pl.ANY)
    vmem_spec = pl.BlockSpec(memory_space=pltpu.VMEM)
    dma = pltpu.SemaphoreType.DMA
    states, scores = pl.pallas_call(
        functools.partial(kernel, n_hist, n_tower),
        out_shape=(
            jax.ShapeDtypeStruct((rows, feat), BF16),
            jax.ShapeDtypeStruct((1, rows), F32),
        ),
        in_specs=[any_spec] * 5 + [pl.BlockSpec(memory_space=pltpu.SMEM)] + [any_spec] * 5,
        out_specs=(vmem_spec, vmem_spec),
        scratch_shapes=[
            pltpu.VMEM((rows, feat), BF16),
            pltpu.VMEM((n_hist, chunks, rows, feat // chunks), BF16),
            pltpu.VMEM((n_hist, 1, rows), jnp.int32),
            pltpu.VMEM(hist_keys.shape, BF16),
            pltpu.VMEM(hist_values.shape, BF16),
            pltpu.VMEM(time_bucket.shape, jnp.int32),
            pltpu.VMEM((rows, feat), BF16),
            pltpu.VMEM(time_bias.shape[::-1], F32),
            pltpu.VMEM((2, feat, hidden), BF16),
            pltpu.VMEM((1, hidden), F32),
            pltpu.VMEM((1, hidden), F32),
            pltpu.VMEM((n_hist, chunks, rows, feat // chunks), BF16),
            pltpu.VMEM((n_hist, chunks, rows, feat // chunks), BF16),
            pltpu.VMEM((2, rows, 128), F32),
            pltpu.VMEM((n_tower, 2, rows, feat), BF16),
            pltpu.VMEM((n_tower, 8, rows), F32),
            pltpu.VMEM((n_tower, 2, 8, rows), F32),
            dma((10,)),
            pltpu.SemaphoreType.REGULAR((n_hist,)),
            dma((2, chunks)),
            dma((n_hist, chunks)),
            dma((n_hist, chunks)),
            dma((n_hist,)),
            dma((n_hist,)),
            dma((n_hist, chunks)),
            dma((n_hist, chunks)),
            dma((2,)),
            dma((2,)),
            dma((2 * n_tower,)),
            dma((n_tower, 2)),
            dma((2 * n_tower,)),
            dma((n_tower, 2)),
        ],
        compiler_params=pltpu.CompilerParams(collective_id=0, has_side_effects=True),
    )(
        queries,
        hist_keys,
        hist_values,
        cand_user.reshape(1, rows),
        time_bucket,
        hist_len,
        cand_gate,
        time_bias.T,
        tower_in,
        tower_bias.reshape(1, -1),
        tower_out.reshape(1, -1),
    )
    states, scores = pl.pallas_call(
        hand_over,
        out_shape=(
            jax.ShapeDtypeStruct((rows, feat), BF16),
            jax.ShapeDtypeStruct((1, rows), F32),
        ),
        in_specs=[vmem_spec, vmem_spec],
        out_specs=(vmem_spec, vmem_spec),
    )(states, scores)
    return states, scores.reshape(rows)


def solution(mesh):
    return jax.shard_map(
        functools.partial(local, n_hist=mesh.shape["hist"], n_tower=mesh.shape["tower"]),
        mesh=mesh,
        in_specs=(
            P(("groups", "hist", "tower"), "head"),
            P("groups", "hist", "head"),
            P("groups", "hist", "head"),
            P(("groups", "hist", "tower")),
            P("groups", "hist"),
            P("groups"),
            P(("groups", "hist", "tower"), "head"),
            P(None, "head"),
            P("head", "tower"),
            P("tower"),
            P("tower"),
        ),
        out_specs=(P(("groups", "hist", "tower"), "head"), P(("groups", "hist", "tower"))),
        check_vma=False,
    )
```
